32 devices in a mesh: seq: 8 (over z, x), head: 4 (over y, core).
Axes of the slice: x: 2, y: 2, z: 4, core: 2. Of those that a mesh axis runs over, the one named last changes fastest.
Arguments:
- x_in: bfloat16 [2048, 4096], P('seq', 'head'), may hold values from -6 to 6
- z_gate: bfloat16 [2048, 4096], P('seq', 'head'), may hold values from -8 to 8
- b_proj: bfloat16 [2048, 4, 256], P('seq', 'head'), may hold values from -6 to 6
- c_proj: bfloat16 [2048, 4, 256], P('seq', 'head'), may hold values from -6 to 6
- log_decay: float32 [2048, 64], P('seq', 'head'), may hold values from -1 to 0
- norm_gain: float32 [4096], P('head'), may hold values from 0.5 to 1.5
- w_out: bfloat16 [4096, 8192], P('head', 'seq'), may hold values from -0.125 to 0.125
Outputs:
- mixed: bfloat16 [2048, 8192], P('seq', 'head')
The draws below stay inside these ranges and needn't reach their ends.
All inputs are finite; a program needn't handle non-finite values.
Results may differ from the reference program's by a relative error of at most 0.015.
Values may be sent and summed in bfloat16 or wider, within the bound.
No kernel may reach another device: no remote copies, remote signals or barrier semaphores. Data moves between devices by JAX's collectives and lax.ppermute only.
A program may use at most 128 MiB of HBM per device.

```python
import math
import jax
import jax.numpy as jnp
from jax import lax

D = 8192
HEAD_DIM = 64
STATE = 256
HEADS_DEV = 16
TOK_DEV = 256
SEQUENCE_LENGTH = 2048
GROUPS = 4
TOTAL_HEADS = 64
INNER = 4096
N_SEQ = 8


def draw_log_decay(key, part):
    key_rows = jax.random.split(jax.random.fold_in(key, 17), 7)
    fast_share = 0.5
    fast = jax.random.uniform(key_rows[0], (1, TOTAL_HEADS)) < fast_share
    slow_rate = jnp.exp(jax.random.uniform(key_rows[1], (1, TOTAL_HEADS), minval=math.log(0.05), maxval=math.log(0.8))) / SEQUENCE_LENGTH
    fast_rate = jnp.exp(jax.random.uniform(key_rows[2], (1, TOTAL_HEADS), minval=math.log(1.0 / 50.0), maxval=math.log(1.0 / 30.0)))
    decay_rate = jnp.where(fast, fast_rate, slow_rate)
    coarse_value = jnp.exp(jax.random.uniform(key_rows[3], (SEQUENCE_LENGTH, TOTAL_HEADS), minval=math.log(0.5), maxval=math.log(2.0)))
    block_list = jnp.exp(jax.random.uniform(key_rows[4], (SEQUENCE_LENGTH // TOK_DEV, 1, TOTAL_HEADS), minval=math.log(0.5), maxval=math.log(2.0)))
    block_list = jnp.broadcast_to(block_list, (SEQUENCE_LENGTH // TOK_DEV, TOK_DEV, TOTAL_HEADS)).reshape(SEQUENCE_LENGTH, TOTAL_HEADS)
    spike_factor = jax.random.randint(key_rows[5], (SEQUENCE_LENGTH, 1), 0, SEQUENCE_LENGTH) < 3
    spike_logarithm = jax.random.uniform(key_rows[6], (SEQUENCE_LENGTH, TOTAL_HEADS), minval=math.log(0.5), maxval=math.log(0.8))
    value_rows = -decay_rate * coarse_value * block_list + jnp.where(spike_factor, spike_logarithm, 0.0)
    return value_rows.astype(jnp.float32)


def raised(array, own_key, source, target, blocks, factor):
    owner, partner = [(jnp.arange(array.shape[position]) // (array.shape[position] // blocks)).reshape([-1 if axis == position else 1 for axis in range(array.ndim)]) for position in (source, target)]
    chosen = jax.random.permutation(own_key, blocks)[partner]
    strong = (owner == chosen) | (owner == (partner + blocks // 2) % blocks)
    return jnp.where(strong, factor * array, array)


def block_levels(stream_key, dims, cuts, low, largest):
    loudness = 1.0
    for position, parts in cuts:
        draws = jax.random.uniform(jax.random.fold_in(jax.random.fold_in(stream_key, 6), position), (parts,), jnp.float32, low / len(cuts), largest / len(cuts))
        loudness = loudness * jnp.repeat(jnp.exp(draws), dims[position] // parts).reshape((-1,) + (1,) * (len(dims) - 1 - position))
    return loudness


def normal_values(stream_key, extent, spread, bound, cuts=(), dtype=jnp.bfloat16):
    values = jax.random.normal(stream_key, extent, jnp.float32) * spread
    if len(cuts) > 0:
        values = block_levels(stream_key, extent, cuts, -0.22, 0.18) * values
    return jnp.clip(values, min=-bound, max=bound).astype(dtype)


def noise_with(stream_key, dims, scale, limit, cuts, heavy, held_as=jnp.bfloat16):
    drawn = scale * jax.random.normal(stream_key, dims, jnp.float32)
    if cuts:
        drawn = drawn * block_levels(stream_key, dims, cuts, -0.22, 0.18)
    return jnp.clip(raised(drawn, jax.random.fold_in(stream_key, 3), *heavy), -limit, limit).astype(held_as)


def setup_inputs(seed: int = 0) -> dict:
    streams_of = jax.random.split(jax.random.key(seed), 8)
    return {
        "x_in": normal_values(streams_of[0], (SEQUENCE_LENGTH, INNER), 1.0, 6.0, ((0, 8), (1, 4))),
        "z_gate": normal_values(streams_of[1], (SEQUENCE_LENGTH, INNER), 1.5, 8.0, ((0, 8), (1, 4))),
        "b_proj": normal_values(streams_of[2], (SEQUENCE_LENGTH, GROUPS, STATE), 1.0, 6.0, ((0, 8), (1, 4))),
        "c_proj": normal_values(streams_of[3], (SEQUENCE_LENGTH, GROUPS, STATE), 1.0, 6.0, ((0, 8), (1, 4))),
        "log_decay": draw_log_decay(jax.random.fold_in(streams_of[7], 71), 0),
        "norm_gain": jnp.clip(0.5 + 1.0 * jax.random.uniform(streams_of[5], (INNER,), jnp.float32) ** block_levels(streams_of[5], (INNER,), ((0, 4),), -0.2, 0.2), 0.5, 1.5),
        "w_out": noise_with(streams_of[6], (INNER, D), INNER ** -0.5, 0.125, ((0, 4), (1, 8)), (0, 1, 8, 2.0)),
    }


def reference(x_in, z_gate, b_proj, c_proj, log_decay, norm_gain, w_out):
    rows = TOK_DEV
    width = HEADS_DEV * HEAD_DIM
    highest = lax.Precision.HIGHEST
    xs = x_in.reshape(N_SEQ, rows, TOTAL_HEADS, HEAD_DIM)
    zs = z_gate.reshape(N_SEQ, rows, INNER)
    bs = b_proj.reshape(N_SEQ, rows, GROUPS, STATE)
    cs = c_proj.reshape(N_SEQ, rows, GROUPS, STATE)
    decays = log_decay.reshape(N_SEQ, rows, TOTAL_HEADS)
    index = jnp.arange(rows)
    causal = (index[:, None] >= index[None, :])[None]
    gains = norm_gain.reshape(GROUPS, width)

    def rounded(value):
        return lax.optimization_barrier(value.astype(jnp.bfloat16)).astype(jnp.float32)

    def step(state, inputs):
        x_blk, z_blk, b_blk, c_blk, l_blk = inputs
        x_f = x_blk.astype(jnp.float32)
        b_f = b_blk.astype(jnp.float32)
        c_f = c_blk.astype(jnp.float32)
        cum = jnp.cumsum(l_blk, axis=0)
        total = cum[-1]
        scores = jnp.einsum('ign,jgn->gij', c_f, b_f, precision=highest)
        scores_h = jnp.repeat(scores, HEADS_DEV, axis=0)
        cum_t = cum.T
        diff = cum_t[:, :, None] - cum_t[:, None, :]
        mask = jnp.where(causal, jnp.exp(jnp.where(causal, diff, 0.0)), 0.0)
        weighted = rounded(mask * scores_h)
        y_intra = jnp.einsum('hij,jhp->ihp', weighted, x_f, precision=highest)
        c_heads = jnp.repeat(c_f, HEADS_DEV, axis=1)
        b_heads = jnp.repeat(b_f, HEADS_DEV, axis=1)
        state_b = rounded(state)
        y_state = jnp.exp(cum)[:, :, None] * jnp.einsum('thn,hpn->thp', c_heads, state_b, precision=highest)
        weights = jnp.exp(total[None, :] - cum)
        scaled = rounded(weights[:, :, None] * x_f)
        new_state = jnp.exp(total)[:, None, None] * state + jnp.einsum('thp,thn->hpn', scaled, b_heads, precision=highest)
        y_all = (y_intra + y_state).reshape(rows, GROUPS, width)
        gated = y_all * jax.nn.silu(z_blk.astype(jnp.float32)).reshape(rows, GROUPS, width)
        mean_sq = lax.optimization_barrier(jnp.mean(gated * gated, axis=2, keepdims=True))
        hidden = (gated * lax.rsqrt(mean_sq + 1e-05) * gains[None]).astype(jnp.bfloat16)
        return (new_state, hidden.reshape(rows, INNER))
    start = jnp.zeros((TOTAL_HEADS, HEAD_DIM, STATE), jnp.float32)
    _, hidden = lax.scan(step, start, (xs, zs, bs, cs, decays))
    hidden = hidden.reshape(SEQUENCE_LENGTH, INNER)
    summed = jnp.zeros((SEQUENCE_LENGTH, D), jnp.float32)
    for group in range(GROUPS):
        partial_term = jnp.dot(hidden[:, group * width:(group + 1) * width], w_out[group * width:(group + 1) * width], preferred_element_type=jnp.float32).astype(jnp.bfloat16)
        partial_term = lax.optimization_barrier(partial_term)
        summed = summed + partial_term.astype(jnp.float32)
    return summed.astype(jnp.bfloat16)
```

```python
import jax
import jax.numpy as jnp
from jax import lax
from jax.sharding import PartitionSpec as P

BF = jnp.bfloat16
F32 = jnp.float32


def decay_rows(decay, width):
    high = decay.astype(BF)
    low = (decay - high.astype(F32)).astype(BF)
    rows = jnp.concatenate([high, low])
    return jnp.broadcast_to(rows[:, None], (rows.shape[0], width))


def pack(state, decay):
    n, p, m = state.shape
    return jnp.concatenate([state.astype(BF).reshape(n * p, m), decay_rows(decay, m)])


def unpack(message, n):
    rows = message.shape[0] - 2 * n
    state = message[:rows].reshape(n, rows // n, -1).astype(F32)
    tail = message[rows:, 0].astype(F32)
    return state, tail[:n] + tail[n:]


def body(x_in, z_gate, b_proj, c_proj, log_decay, norm_gain, w_out):
    rows = x_in.shape[0]
    heads = log_decay.shape[1]
    head_dim = x_in.shape[1] // heads
    n_seq, n_head = lax.axis_size("seq"), lax.axis_size("head")
    r = n_seq // n_head
    n_y = n_head // 2
    me_seq, me_head = lax.axis_index("seq"), lax.axis_index("head")
    me_h, me_b = me_seq // r, me_seq % r

    def rot_b(v, j):
        pairs = [(h * r + b, h * r + (b + j) % r) for h in range(n_head) for b in range(r)]
        return lax.ppermute(v, "seq", pairs)

    def rot_h(v, k):
        pairs = [(h * r + b, (h + k) % n_head * r + b) for h in range(n_head) for b in range(r)]
        return lax.ppermute(v, "seq", pairs)

    def shift_h(v, k):
        pairs = [(h * r + b, (h + k) * r + b) for h in range(n_head - k) for b in range(r)]
        return lax.ppermute(v, "seq", pairs)

    def swap_core(v):
        return lax.ppermute(v, "head", [(i, i ^ 1) for i in range(n_head)])

    def rot_y(v, j):
        pairs = [(y * 2 + c, (y + j) % n_y * 2 + c) for y in range(n_y) for c in range(2)]
        return lax.ppermute(v, "head", pairs)

    def rot_head(v, j):
        return lax.ppermute(v, "head", [(i, (i + j) % n_head) for i in range(n_head)])

    pick = lambda v, i: lax.dynamic_index_in_dim(v, i, 0, keepdims=False)
    core = me_head % 2

    b_local = b_proj[:, 0, :]
    c_local = c_proj[:, 0, :]
    x_heads = x_in.reshape(rows, heads, head_dim)
    cum = jnp.cumsum(log_decay, axis=0)
    total = cum[-1]
    weights = jnp.exp(total[None, :] - cum)
    scaled = (weights[:, :, None] * x_heads.astype(F32)).astype(BF)
    state = jnp.einsum("thp,tn->hpn", scaled, b_local, preferred_element_type=F32)
    decay = jnp.exp(total)

    part = heads // r
    groups = jnp.stack(
        [pack(state[j * part : (j + 1) * part], decay[j * part : (j + 1) * part]) for j in range(r)]
    )
    got = [pick(groups, me_b)]
    for j in range(1, r):
        got.append(rot_b(pick(groups, (me_b + j) % r), j))
    got = jnp.stack(got)
    blocks = [unpack(pick(got, (me_b - i) % r), part) for i in range(r)]
    scale = lambda d, s: d[:, None, None] * s
    run, run_decay = blocks[0]
    for s, d in blocks[1:]:
        run, run_decay = scale(d, run) + s, d * run_decay
    before, before_decay = jnp.zeros_like(run), jnp.ones_like(run_decay)
    k = 1
    while k < n_head:
        s, d = unpack(shift_h(pack(run, run_decay), k), part)
        before, before_decay = before + scale(before_decay, s), before_decay * d
        run, run_decay = run + scale(run_decay, s), run_decay * d
        k *= 2
    entering = []
    for s, d in blocks:
        entering.append(before.astype(BF))
        before = scale(d, before) + s
    entering = jnp.stack(entering)
    back = [pick(entering, me_b)]
    for j in range(1, r):
        back.append(rot_b(pick(entering, (me_b + j) % r), j))
    back = jnp.stack(back)
    state_in = jnp.concatenate([pick(back, (me_b - i) % r) for i in range(r)])

    width = w_out.shape[1] // 2
    halves = jnp.stack([w_out[:, :width], w_out[:, width:]])
    w_mine = pick(halves, core)
    w_other = swap_core(pick(halves, 1 - core))
    w_pieces = [(w_mine, w_other)]
    for j in range(1, r):
        w_pieces.append((rot_b(w_mine, j), rot_b(w_other, j)))

    scores = jnp.dot(c_local, b_local.T, preferred_element_type=F32)
    index = jnp.arange(rows)
    causal = (index[:, None] >= index[None, :])[None]
    cum_t = cum.T
    diff = cum_t[:, :, None] - cum_t[:, None, :]
    mask = jnp.where(causal, jnp.exp(jnp.where(causal, diff, 0.0)), 0.0)
    weighted = (mask * scores[None]).astype(BF)
    y_intra = jnp.einsum("hij,jhp->ihp", weighted, x_heads, preferred_element_type=F32)
    y_state = jnp.exp(cum)[:, :, None] * jnp.einsum(
        "tn,hpn->thp", c_local, state_in, preferred_element_type=F32
    )
    y_all = (y_intra + y_state).reshape(rows, heads * head_dim)
    gated = y_all * jax.nn.silu(z_gate.astype(F32))
    mean_sq = jnp.mean(gated * gated, axis=1, keepdims=True)
    hidden = (gated * lax.rsqrt(mean_sq + 1e-05) * norm_gain[None, :]).astype(BF)

    piece = rows // n_y
    me_y = me_head // 2
    home = []
    for k in range(n_head):
        if k:
            hidden = rot_h(hidden, 1)
        other = swap_core(hidden)
        terms = [
            jnp.dot(hidden, w0, preferred_element_type=F32)
            + jnp.dot(other, w1, preferred_element_type=F32)
            for w0, w1 in w_pieces
        ]
        terms = jnp.stack(terms).reshape(r, n_y, piece, width)
        mine = lax.dynamic_index_in_dim(terms, me_y, 1, keepdims=False)
        for j in range(1, n_y):
            send = lax.dynamic_index_in_dim(terms, (me_y + j) % n_y, 1, keepdims=False)
            mine = mine + rot_y(send.astype(BF), j).astype(F32)
        mine = mine.astype(BF)
        home.append(rot_h(mine, -k) if k else mine)
    home = jnp.stack(home)
    final = [pick(home, (me_head - me_h) % n_head)]
    for j in range(1, n_head):
        final.append(rot_head(pick(home, (me_head + j - me_h) % n_head), j))
    final = jnp.stack(final)
    final = jnp.stack([pick(final, (me_head - i) % n_head) for i in range(n_head)])
    final = jnp.stack([lax.dynamic_index_in_dim(final, (me_b - i) % r, 1, False) for i in range(r)])
    final = final.reshape(r, n_y, 2, piece, width)
    return final.transpose(1, 3, 0, 2, 4).reshape(rows, r * 2 * width)


def solution(mesh):
    placed = (
        P("seq", "head"),
        P("seq", "head"),
        P("seq", "head", None),
        P("seq", "head", None),
        P("seq", "head"),
        P("head"),
        P("head", "seq"),
    )
    return jax.shard_map(
        body, mesh=mesh, in_specs=placed, out_specs=P("seq", "head"), check_vma=False
    )
```

```python
import functools
import jax
import jax.numpy as jnp
from jax import lax
from jax.experimental import pallas as pl
from jax.experimental.pallas import tpu as pltpu
from jax.sharding import PartitionSpec as P

BF = jnp.bfloat16
F32 = jnp.float32
HIGH = lax.Precision.HIGHEST
TAIL = 16
CHUNKS = 2
MINE, OTHER, EARLY = (4, 4), (3, 5), 3


def call(kernel, out_shapes, args, scratch=(), traffic=1, resident=0):
    vmem = pl.BlockSpec(memory_space=pltpu.VMEM)
    any_ = pl.BlockSpec()
    smem = pl.BlockSpec(memory_space=pltpu.SMEM)
    outs = pl.pallas_call(
        kernel,
        out_shape=[jax.ShapeDtypeStruct(s, d) for s, d in out_shapes],
        in_specs=[smem] + [any_] * (len(args) - 1 - resident) + [vmem] * resident,
        out_specs=[any_] * len(out_shapes),
        scratch_shapes=list(scratch),
        compiler_params=pltpu.CompilerParams(vmem_limit_bytes=16 << 20),
        cost_estimate=pl.CostEstimate(flops=1, transcendentals=0, bytes_accessed=traffic),
    )(*args)
    return list(outs)


def triangle(rows):
    i = lax.broadcasted_iota(jnp.int32, (rows, rows), 0)
    j = lax.broadcasted_iota(jnp.int32, (rows, rows), 1)
    return i >= j


def spread(per_head, channels):
    heads = per_head.shape[1]
    h = lax.broadcasted_iota(jnp.int32, (heads, channels), 0)
    c = lax.broadcasted_iota(jnp.int32, (heads, channels), 1)
    pick = (c // (channels // heads) == h).astype(F32)
    return jnp.dot(per_head, pick, precision=HIGH, preferred_element_type=F32)


def write_message(ref, state, decay):
    n, w = state.shape
    ref[0:n, :] = state.astype(BF)
    high = decay.astype(BF).astype(F32)
    row = lax.broadcasted_iota(jnp.int32, (TAIL, w), 0)
    tail = jnp.where(row < TAIL // 2, high, decay - high)
    ref[n : n + TAIL, :] = tail.astype(BF)


def read_message(ref):
    n = ref.shape[0] - TAIL
    tail = ref[n : n + TAIL, :].astype(F32)
    return ref[0:n, :].astype(F32), tail[0:1] + tail[TAIL // 2 : TAIL // 2 + 1]


def state_kernel(r, me, x, b, logs, keep, *sends):
    rows, channels = x.shape
    tri = triangle(rows).astype(F32)
    cum = jnp.dot(tri, logs[...], precision=HIGH, preferred_element_type=F32)
    total = cum[rows - 1 : rows, :]
    weights = spread(jnp.exp(total - cum), channels)
    decay = spread(jnp.broadcast_to(jnp.exp(total), (8, total.shape[1])), channels)[0:1]
    scaled = (weights * x[...].astype(F32)).astype(BF)
    state = lax.dot_general(b[...], scaled, (((0,), (0,)), ((), ())), preferred_element_type=F32)
    w = channels // r
    for g in range(r):

        @pl.when(me[0] == g)
        def _():
            for j, ref in enumerate((keep,) + sends):
                at = (g + j) % r * w
                write_message(ref, state[:, at : at + w], decay[:, at : at + w])


def fold_kernel(r, me, *refs):
    got, (message, run, run_decay) = refs[:r], refs[r:]
    for g in range(r):

        @pl.when(me[0] == g)
        def _():
            total, decay = read_message(got[g])
            for i in range(1, r):
                s, d = read_message(got[(g - i) % r])
                total, decay = total * d + s, decay * d
            write_message(message, total, decay)
            run[...] = total
            run_decay[...] = jnp.broadcast_to(decay, run_decay.shape)


def step_kernel(first, me, got, before, before_decay, run, run_decay, message, o_before, o_before_decay, o_run, o_run_decay):
    s, d = read_message(got)
    if first:
        o_before[...], o_before_decay[...] = s, jnp.broadcast_to(d, o_before_decay.shape)
    else:
        o_before[...] = before[...] + before_decay[0:1] * s
        o_before_decay[...] = before_decay[...] * d
    total = run[...] + run_decay[0:1] * s
    decay = run_decay[0:1] * d
    write_message(message, total, decay)
    o_run[...] = total
    o_run_decay[...] = jnp.broadcast_to(decay, o_run_decay.shape)


def enter_kernel(r, me, got, before, before_decay, *refs):
    blocks, outs = refs[:r], refs[r:]
    s, _ = read_message(got)
    start = before[...] + before_decay[0:1] * s
    for g in range(r):

        @pl.when(me[0] == g)
        def _():
            now = start
            for i in range(r):
                outs[(i - g) % r][...] = now.astype(BF)
                if i + 1 < r:
                    q, d = read_message(blocks[(g - i) % r])
                    now = now * d + q


def within_kernel(me, x, z, b, c, logs, y, silu, grow):
    rows, channels = x.shape
    heads = logs.shape[1]
    width = channels // heads
    causal = triangle(rows)
    tri = causal.astype(F32)
    cum = jnp.dot(tri, logs[...], precision=HIGH, preferred_element_type=F32)
    cum_t = lax.dot_general(
        logs[...], tri, (((0,), (1,)), ((), ())), precision=HIGH, preferred_element_type=F32
    )
    scores = lax.dot_general(
        c[...], b[...], (((1,), (1,)), ((), ())), preferred_element_type=F32
    )
    scores = jnp.where(causal, scores, 0.0)
    for h in range(heads):
        diff = cum[:, h : h + 1] - cum_t[h : h + 1, :]
        mask = jnp.exp(jnp.where(causal, diff, 0.0))
        weighted = (mask * scores).astype(BF)
        at = slice(h * width, (h + 1) * width)
        y[:, at] = jnp.dot(weighted, x[:, at], preferred_element_type=F32)
    gate = z[...].astype(F32)
    silu[...] = gate / (1.0 + jnp.exp(-gate))
    grow[...] = spread(jnp.exp(cum), channels)


def hidden_kernel(r, me, c, y, silu, grow, gain, *refs):
    parts, outs, entering = refs[:r], refs[r:-1], refs[-1]
    w = entering.shape[1] // r
    for g in range(r):

        @pl.when(me[0] == g)
        def _():
            for j in range(r):
                at = (g - j) % r * w
                entering[:, at : at + w] = parts[j][...]

    rows = c.shape[0] // len(outs)
    for i, out in enumerate(outs):
        at = slice(i * rows, (i + 1) * rows)
        carried = jnp.dot(c[at, :], entering[...], preferred_element_type=F32)
        gated = (y[at, :] + grow[at, :] * carried) * silu[at, :]
        mean_sq = jnp.mean(gated * gated, axis=1, keepdims=True)
        out[...] = (gated * lax.rsqrt(mean_sq + 1e-05) * gain[...]).astype(BF)


def split_kernel(n_mine, core, w_out, *refs):
    width = refs[0].shape[1]
    for g in range(2):

        @pl.when(core[0] == g)
        def _():
            for parts, side in ((refs[:n_mine], g), (refs[n_mine:], 1 - g)):
                at = 0
                for ref in parts:
                    rows = ref.shape[0]
                    ref[...] = w_out[at : at + rows, side * width : (side + 1) * width]
                    at += rows


def product_kernel(r, n_y, chunks, me, *refs):
    rows = [jnp.concatenate([ref[...] for ref in refs[i * chunks : (i + 1) * chunks]]) for i in range(2)]
    weights, (mine, *sends) = refs[2 * chunks : -n_y], refs[-n_y:]
    per = len(weights) // r
    shares = [ref.shape[0] for ref in weights[:per]]
    half = rows[0].shape[0] // chunks
    part = half // n_y
    for p in range(r):
        term, side, at = None, 0, 0
        for ref, share in zip(weights[p * per : (p + 1) * per], shares):
            one = jnp.dot(
                rows[side][:, at : at + share], ref[...], preferred_element_type=F32
            )
            term = one if term is None else term + one
            at += share
            if at == rows[0].shape[1]:
                side, at = 1, 0
        for g in range(n_y):

            @pl.when(me[0] == g)
            def _():
                for i in range(chunks):
                    at = i * half + g * part
                    mine[i, p] = term[at : at + part]
                    for j, ref in enumerate(sends):
                        at = i * half + (g + j + 1) % n_y * part
                        ref[i, p] = term[at : at + part].astype(BF)


def sum_kernel(me, mine, *refs):
    gots, out = refs[:-1], refs[-1]
    total = mine[...]
    for got in gots:
        total = total + got[...].astype(F32)
    out[...] = total.astype(BF)


def turn_kernel(n, chunk, by, *refs):
    ins, outs = refs[:n], refs[n:]
    for g in range(n):

        @pl.when(by[0] == g)
        def _():
            for j in range(n):
                ref = ins[(g + j) % n]
                outs[j][...] = ref[chunk if ref.shape[0] > 1 else 0]


def gather_kernel(n, me, *refs):
    ins, out = refs[:-1], refs[-1]
    r, part, width = ins[0].shape
    for t, ref in enumerate(ins):
        i, j = t // n, t % n
        source = lax.rem(me[0] + n - j, n)
        row = i * (n // 2) * part + lax.div(source, 2) * part
        row = pl.multiple_of(row, part)
        for p in range(r):
            order = lax.rem(me[1] + r - p, r)
            column = pl.multiple_of((2 * order + lax.rem(source, 2)) * width, width)
            out[pl.ds(row, part), pl.ds(column, width)] = ref[p]


def body(x_in, z_gate, b_proj, c_proj, log_decay, norm_gain, w_out):
    rows, channels = x_in.shape
    n_seq, n_head = lax.axis_size("seq"), lax.axis_size("head")
    r = n_seq // n_head
    n_y = n_head // 2
    me_seq, me_head = lax.axis_index("seq"), lax.axis_index("head")
    me_h, me_b = me_seq // r, me_seq % r
    me = me_b.reshape(1)

    def rot_b(v, j):
        pairs = [(h * r + b, h * r + (b + j) % r) for h in range(n_head) for b in range(r)]
        return lax.ppermute(v, "seq", pairs)

    def rot_h(v, k):
        pairs = [(h * r + b, (h + k) % n_head * r + b) for h in range(n_head) for b in range(r)]
        return lax.ppermute(v, "seq", pairs)

    def shift_h(v, k):
        pairs = [(h * r + b, (h + k) * r + b) for h in range(n_head - k) for b in range(r)]
        return lax.ppermute(v, "seq", pairs)

    def swap_core(v):
        return lax.ppermute(v, "head", [(i, i ^ 1) for i in range(n_head)])

    def rot_y(v, j):
        pairs = [(y * 2 + c, (y + j) % n_y * 2 + c) for y in range(n_y) for c in range(2)]
        return lax.ppermute(v, "head", pairs)

    def rot_head(v, j):
        return lax.ppermute(v, "head", [(i, (i + j) % n_head) for i in range(n_head)])

    pick = lambda v, i: lax.dynamic_index_in_dim(v, i, 0, keepdims=False)
    after = lambda v, *first: lax.optimization_barrier((v,) + first)[0]
    core = (me_head % 2).reshape(1)
    b_local = b_proj[:, 0, :]
    c_local = c_proj[:, 0, :]
    n = b_local.shape[1]
    w = channels // r
    message = ((n + TAIL, w), BF)
    full, row = ((n, w), F32), ((8, w), F32)

    sends = call(functools.partial(state_kernel, r), [message] * r, (me, x_in, b_local, log_decay))
    got = [sends[0]] + [rot_b(sends[j], j) for j in range(1, r)]
    depth, width = w_out.shape[0], w_out.shape[1] // 2
    mine_rows, other_rows = [[depth * i // 8 for i in cut] for cut in (MINE, OTHER)]
    split = call(
        functools.partial(split_kernel, len(mine_rows)),
        [((d, width), BF) for d in mine_rows + other_rows],
        (core, after(w_out, *sends)),
        traffic=4 * w_out.size * w_out.dtype.itemsize,
    )
    w_own = split[: len(mine_rows)] + [swap_core(v) for v in split[len(mine_rows) :]]
    w_parts = [w_own]
    for j in range(1, r):
        w_parts.append([rot_b(v, j) for v in w_own[:EARLY]])
    early = [v for group in w_parts[1:] for v in group]
    out, run, run_decay = call(functools.partial(fold_kernel, r), [message, full, row], (me, *got))
    before, before_decay = run, run_decay
    out = after(out, *split)
    k = 1
    while 2 * k < n_head:
        out, before, before_decay, run, run_decay = call(
            functools.partial(step_kernel, k == 1),
            [message, full, row, full, row],
            (me, shift_h(out, k), before, before_decay, run, run_decay),
        )
        k *= 2
        out = after(out, *[group[0] for group in w_parts[1:]])
    entering = call(
        functools.partial(enter_kernel, r),
        [((n, w), BF)] * r,
        (me, shift_h(out, k), before, before_decay, *got),
    )
    parts = [entering[0]] + [rot_b(after(entering[j], *early), j) for j in range(1, r)]
    y, silu, grow = call(
        within_kernel,
        [((rows, channels), F32)] * 3,
        (me, x_in, after(z_gate, *entering), b_local, c_local, log_decay),
    )
    part_rows = rows // CHUNKS
    hidden = call(
        functools.partial(hidden_kernel, r),
        [((part_rows, channels), BF)] * CHUNKS,
        (me, c_local, y, silu, grow, norm_gain.reshape(1, channels), *parts),
        scratch=[pltpu.VMEM((n, channels), BF)],
    )

    for j in range(1, r):
        w_parts[j].extend(rot_b(after(v, y), j) for v in w_own[EARLY:])
    weights = [v for group in w_parts for v in group]

    piece = part_rows // n_y
    me_y = (me_head // 2).reshape(1)
    steps = [(k, list(range(CHUNKS))) for k in range(n_head - 1)]
    steps += [(n_head - 1, [i]) for i in range(CHUNKS)]
    hidden = list(hidden)
    home, sums, back, outs = [[] for _ in range(CHUNKS)], [], [], []
    for t, (k, chunks) in enumerate(steps):
        now = [hidden[i] for i in chunks]
        if k + 1 < n_head:
            hidden = [rot_h(after(v, *outs[: max(t - 1, 0)]), 1) for v in hidden]
        other = [swap_core(v) for v in now]
        if t > 1:
            other[0] = after(other[0], sums[t - 2], *back[: max(t - 3, 0)])
        shape = (len(chunks), r, piece, width)
        mine, *send = call(
            functools.partial(product_kernel, r, n_y, len(chunks)),
            [(shape, F32)] + [(shape, BF)] * (n_y - 1),
            (me_y, *now, *other, *weights),
            resident=len(weights),
        )
        outs.append(mine)
        gots = [rot_y(v, j + 1) for j, v in enumerate(send)]
        (last,) = call(sum_kernel, [(shape, BF)], (me_y, mine, *gots))
        sums.append(last)
        if k:
            last = rot_h(last, -k)
            back.append(last)
        for i in chunks:
            home[i].append(last)
    by = lax.rem(me_head + n_head - me_h, n_head).reshape(1)
    pieces = []
    for i in range(CHUNKS):
        ready = call(
            functools.partial(turn_kernel, n_head, i),
            [((r, piece, width), BF)] * n_head,
            (by, *home[i]),
        )
        pieces.append(ready[0])
        pieces.extend(rot_head(ready[j], j) for j in range(1, n_head))
    (out,) = call(
        functools.partial(gather_kernel, n_head),
        [((rows, r * 2 * width), BF)],
        (jnp.stack([me_head, me_b]), *pieces),
    )
    return out


def solution(mesh):
    placed = (
        P("seq", "head"),
        P("seq", "head"),
        P("seq", "head", None),
        P("seq", "head", None),
        P("seq", "head"),
        P("head"),
        P("head", "seq"),
    )
    return jax.shard_map(
        body, mesh=mesh, in_specs=placed, out_specs=P("seq", "head"), check_vma=False
    )
```

```python
import functools
import jax
import jax.numpy as jnp
from jax import lax
from jax.experimental import pallas as pl
from jax.experimental.pallas import tpu as pltpu
from jax.sharding import PartitionSpec as P

BF = jnp.bfloat16
F32 = jnp.float32
HIGH = lax.Precision.HIGHEST
TAIL = 16
CHUNKS = 2
MINE, OTHER, EARLY = (4, 4), (3, 5), 3


def call(kernel, out_shapes, args, scratch=(), traffic=1, resident=0):
    vmem = pl.BlockSpec(memory_space=pltpu.VMEM)
    any_ = pl.BlockSpec()
    smem = pl.BlockSpec(memory_space=pltpu.SMEM)
    outs = pl.pallas_call(
        kernel,
        out_shape=[jax.ShapeDtypeStruct(s, d) for s, d in out_shapes],
        in_specs=[smem] + [any_] * (len(args) - 1 - resident) + [vmem] * resident,
        out_specs=[any_] * len(out_shapes),
        scratch_shapes=list(scratch),
        compiler_params=pltpu.CompilerParams(vmem_limit_bytes=16 << 20),
        cost_estimate=pl.CostEstimate(flops=1, transcendentals=0, bytes_accessed=traffic),
    )(*args)
    return list(outs)


def triangle(rows):
    i = lax.broadcasted_iota(jnp.int32, (rows, rows), 0)
    j = lax.broadcasted_iota(jnp.int32, (rows, rows), 1)
    return i >= j


def spread(per_head, channels):
    heads = per_head.shape[1]
    h = lax.broadcasted_iota(jnp.int32, (heads, channels), 0)
    c = lax.broadcasted_iota(jnp.int32, (heads, channels), 1)
    pick = (c // (channels // heads) == h).astype(F32)
    return jnp.dot(per_head, pick, precision=HIGH, preferred_element_type=F32)


def write_message(ref, state, decay):
    n, w = state.shape
    ref[0:n, :] = state.astype(BF)
    high = decay.astype(BF).astype(F32)
    row = lax.broadcasted_iota(jnp.int32, (TAIL, w), 0)
    tail = jnp.where(row < TAIL // 2, high, decay - high)
    ref[n : n + TAIL, :] = tail.astype(BF)


def read_message(ref):
    n = ref.shape[0] - TAIL
    tail = ref[n : n + TAIL, :].astype(F32)
    return ref[0:n, :].astype(F32), tail[0:1] + tail[TAIL // 2 : TAIL // 2 + 1]


def state_kernel(r, me, x, b, logs, keep, *sends):
    rows, channels = x.shape
    tri = triangle(rows).astype(F32)
    cum = jnp.dot(tri, logs[...], precision=HIGH, preferred_element_type=F32)
    total = cum[rows - 1 : rows, :]
    weights = spread(jnp.exp(total - cum), channels)
    decay = spread(jnp.broadcast_to(jnp.exp(total), (8, total.shape[1])), channels)[0:1]
    scaled = (weights * x[...].astype(F32)).astype(BF)
    state = lax.dot_general(b[...], scaled, (((0,), (0,)), ((), ())), preferred_element_type=F32)
    w = channels // r
    for g in range(r):

        @pl.when(me[0] == g)
        def _():
            for j, ref in enumerate((keep,) + sends):
                at = (g + j) % r * w
                write_message(ref, state[:, at : at + w], decay[:, at : at + w])


def fold_kernel(r, me, *refs):
    got, (message, run, run_decay) = refs[:r], refs[r:]
    for g in range(r):

        @pl.when(me[0] == g)
        def _():
            total, decay = read_message(got[g])
            for i in range(1, r):
                s, d = read_message(got[(g - i) % r])
                total, decay = total * d + s, decay * d
            write_message(message, total, decay)
            run[...] = total
            run_decay[...] = jnp.broadcast_to(decay, run_decay.shape)


def step_kernel(first, me, got, before, before_decay, run, run_decay, *refs):
    message, o_before, o_before_decay, o_run, o_run_decay = refs[-5:]
    s, d = read_message(got)
    if first:
        o_before[...], o_before_decay[...] = s, jnp.broadcast_to(d, o_before_decay.shape)
    else:
        o_before[...] = before[...] + before_decay[0:1] * s
        o_before_decay[...] = before_decay[...] * d
    total = run[...] + run_decay[0:1] * s
    decay = run_decay[0:1] * d
    write_message(message, total, decay)
    o_run[...] = total
    o_run_decay[...] = jnp.broadcast_to(decay, o_run_decay.shape)


def enter_kernel(r, me, got, before, before_decay, *refs):
    blocks, outs = refs[:r], refs[r:]
    s, _ = read_message(got)
    start = before[...] + before_decay[0:1] * s
    for g in range(r):

        @pl.when(me[0] == g)
        def _():
            now = start
            for i in range(r):
                outs[(i - g) % r][...] = now.astype(BF)
                if i + 1 < r:
                    q, d = read_message(blocks[(g - i) % r])
                    now = now * d + q


def within_kernel(me, x, z, b, c, logs, y, silu, grow):
    rows, channels = x.shape
    heads = logs.shape[1]
    width = channels // heads
    causal = triangle(rows)
    tri = causal.astype(F32)
    cum = jnp.dot(tri, logs[...], precision=HIGH, preferred_element_type=F32)
    cum_t = lax.dot_general(
        logs[...], tri, (((0,), (1,)), ((), ())), precision=HIGH, preferred_element_type=F32
    )
    scores = lax.dot_general(
        c[...], b[...], (((1,), (1,)), ((), ())), preferred_element_type=F32
    )
    scores = jnp.where(causal, scores, 0.0)
    for h in range(heads):
        diff = cum[:, h : h + 1] - cum_t[h : h + 1, :]
        mask = jnp.exp(jnp.where(causal, diff, 0.0))
        weighted = (mask * scores).astype(BF)
        at = slice(h * width, (h + 1) * width)
        y[:, at] = jnp.dot(weighted, x[:, at], preferred_element_type=F32)
    gate = z[...].astype(F32)
    silu[...] = gate / (1.0 + jnp.exp(-gate))
    grow[...] = spread(jnp.exp(cum), channels)


def hidden_kernel(r, me, c, y, silu, grow, gain, *refs):
    parts, outs, entering = refs[:r], refs[-1 - CHUNKS : -1], refs[-1]
    w = entering.shape[1] // r
    for g in range(r):

        @pl.when(me[0] == g)
        def _():
            for j in range(r):
                at = (g - j) % r * w
                entering[:, at : at + w] = parts[j][...]

    rows = c.shape[0] // len(outs)
    for i, out in enumerate(outs):
        at = slice(i * rows, (i + 1) * rows)
        carried = jnp.dot(c[at, :], entering[...], preferred_element_type=F32)
        gated = (y[at, :] + grow[at, :] * carried) * silu[at, :]
        mean_sq = jnp.mean(gated * gated, axis=1, keepdims=True)
        out[...] = (gated * lax.rsqrt(mean_sq + 1e-05) * gain[...]).astype(BF)


def split_kernel(n_mine, core, w_out, *refs):
    width = refs[0].shape[1]
    for g in range(2):

        @pl.when(core[0] == g)
        def _():
            for parts, side in ((refs[:n_mine], g), (refs[n_mine:], 1 - g)):
                at = 0
                for ref in parts:
                    rows = ref.shape[0]
                    ref[...] = w_out[at : at + rows, side * width : (side + 1) * width]
                    at += rows


def product_kernel(r, n_y, chunks, me, *refs):
    rows = [jnp.concatenate([ref[...] for ref in refs[i * chunks : (i + 1) * chunks]]) for i in range(2)]
    weights, (mine, *sends) = refs[2 * chunks : -n_y], refs[-n_y:]
    per = len(weights) // r
    shares = [ref.shape[0] for ref in weights[:per]]
    half = rows[0].shape[0] // chunks
    part = half // n_y
    for p in range(r):
        term, side, at = None, 0, 0
        for ref, share in zip(weights[p * per : (p + 1) * per], shares):
            one = jnp.dot(
                rows[side][:, at : at + share], ref[...], preferred_element_type=F32
            )
            term = one if term is None else term + one
            at += share
            if at == rows[0].shape[1]:
                side, at = 1, 0
        for g in range(n_y):

            @pl.when(me[0] == g)
            def _():
                for i in range(chunks):
                    at = i * half + g * part
                    mine[i, p] = term[at : at + part]
                    for j, ref in enumerate(sends):
                        at = i * half + (g + j + 1) % n_y * part
                        ref[i, p] = term[at : at + part].astype(BF)


def sum_kernel(me, mine, *refs):
    gots, out = refs[:-1], refs[-1]
    total = mine[...]
    for got in gots:
        total = total + got[...].astype(F32)
    out[...] = total.astype(BF)


def turn_kernel(n, chunk, by, *refs):
    ins, outs = refs[:n], refs[n:]
    for g in range(n):

        @pl.when(by[0] == g)
        def _():
            for j in range(n):
                ref = ins[(g + j) % n]
                outs[j][...] = ref[chunk if ref.shape[0] > 1 else 0]


def gather_kernel(n, me, *refs):
    ins, out = refs[:-1], refs[-1]
    r, part, width = ins[0].shape
    for t, ref in enumerate(ins):
        i, j = t // n, t % n
        source = lax.rem(me[0] + n - j, n)
        row = i * (n // 2) * part + lax.div(source, 2) * part
        row = pl.multiple_of(row, part)
        for p in range(r):
            order = lax.rem(me[1] + r - p, r)
            column = pl.multiple_of((2 * order + lax.rem(source, 2)) * width, width)
            out[pl.ds(row, part), pl.ds(column, width)] = ref[p]


def body(x_in, z_gate, b_proj, c_proj, log_decay, norm_gain, w_out):
    rows, channels = x_in.shape
    n_seq, n_head = lax.axis_size("seq"), lax.axis_size("head")
    r = n_seq // n_head
    n_y = n_head // 2
    me_seq, me_head = lax.axis_index("seq"), lax.axis_index("head")
    me_h, me_b = me_seq // r, me_seq % r
    me = me_b.reshape(1)

    def rot_b(v, j):
        pairs = [(h * r + b, h * r + (b + j) % r) for h in range(n_head) for b in range(r)]
        return lax.ppermute(v, "seq", pairs)

    def rot_h(v, k):
        pairs = [(h * r + b, (h + k) % n_head * r + b) for h in range(n_head) for b in range(r)]
        return lax.ppermute(v, "seq", pairs)

    def shift_h(v, k):
        pairs = [(h * r + b, (h + k) * r + b) for h in range(n_head - k) for b in range(r)]
        return lax.ppermute(v, "seq", pairs)

    def swap_core(v):
        return lax.ppermute(v, "head", [(i, i ^ 1) for i in range(n_head)])

    def rot_y(v, j):
        pairs = [(y * 2 + c, (y + j) % n_y * 2 + c) for y in range(n_y) for c in range(2)]
        return lax.ppermute(v, "head", pairs)

    def rot_head(v, j):
        return lax.ppermute(v, "head", [(i, (i + j) % n_head) for i in range(n_head)])

    pick = lambda v, i: lax.dynamic_index_in_dim(v, i, 0, keepdims=False)
    after = lambda v, *first: lax.optimization_barrier((v,) + first)[0]
    core = (me_head % 2).reshape(1)
    b_local = b_proj[:, 0, :]
    c_local = c_proj[:, 0, :]
    n = b_local.shape[1]
    w = channels // r
    message = ((n + TAIL, w), BF)
    full, row = ((n, w), F32), ((8, w), F32)

    sends = call(functools.partial(state_kernel, r), [message] * r, (me, x_in, b_local, log_decay))
    got = [sends[0]] + [rot_b(sends[j], j) for j in range(1, r)]
    depth, width = w_out.shape[0], w_out.shape[1] // 2
    mine_rows, other_rows = [[depth * i // 8 for i in cut] for cut in (MINE, OTHER)]
    split = call(
        functools.partial(split_kernel, len(mine_rows)),
        [((d, width), BF) for d in mine_rows + other_rows],
        (core, after(w_out, *sends)),
        traffic=4 * w_out.size * w_out.dtype.itemsize,
    )
    w_own = split[: len(mine_rows)] + [swap_core(v) for v in split[len(mine_rows) :]]
    w_parts = [w_own]
    for j in range(1, r):
        w_parts.append([rot_b(v, j) for v in w_own[:EARLY]])
    early = [v for group in w_parts[1:] for v in group]
    out, run, run_decay = call(functools.partial(fold_kernel, r), [message, full, row], (me, *got))
    before, before_decay = run, run_decay
    out = after(out, *split)
    k = 1
    while 2 * k < n_head:
        out, before, before_decay, run, run_decay = call(
            functools.partial(step_kernel, k == 1),
            [message, full, row, full, row],
            (me, shift_h(out, k), before, before_decay, run, run_decay, *got),
        )
        k *= 2
        out = after(out, *[group[0] for group in w_parts[1:]])
    entering = call(
        functools.partial(enter_kernel, r),
        [((n, w), BF)] * r,
        (me, shift_h(out, k), before, before_decay, *got),
    )
    parts = [entering[0]] + [rot_b(after(entering[j], *early), j) for j in range(1, r)]
    y, silu, grow = call(
        within_kernel,
        [((rows, channels), F32)] * 3,
        (me, x_in, after(z_gate, *entering), b_local, c_local, log_decay),
    )
    part_rows = rows // CHUNKS
    hidden = call(
        functools.partial(hidden_kernel, r),
        [((part_rows, channels), BF)] * CHUNKS,
        (me, c_local, y, silu, grow, norm_gain.reshape(1, channels), *parts, *early),
        scratch=[pltpu.VMEM((n, channels), BF)],
    )

    for j in range(1, r):
        w_parts[j].extend(rot_b(after(v, y), j) for v in w_own[EARLY:])
    weights = [v for group in w_parts for v in group]

    piece = part_rows // n_y
    me_y = (me_head // 2).reshape(1)
    steps = [(k, list(range(CHUNKS))) for k in range(n_head - 1)]
    steps += [(n_head - 1, [i]) for i in range(CHUNKS)]
    hidden = list(hidden)
    home, sums, back, outs = [[] for _ in range(CHUNKS)], [], [], []
    for t, (k, chunks) in enumerate(steps):
        now = [hidden[i] for i in chunks]
        if k + 1 < n_head:
            hidden = [rot_h(after(v, *outs[: max(t - 1, 0)]), 1) for v in hidden]
        other = [swap_core(v) for v in now]
        if t > 2:
            other[0] = after(other[0], sums[t - 3])
        shape = (len(chunks), r, piece, width)
        mine, *send = call(
            functools.partial(product_kernel, r, n_y, len(chunks)),
            [(shape, F32)] + [(shape, BF)] * (n_y - 1),
            (me_y, *now, *other, *weights),
            resident=len(weights),
        )
        outs.append(mine)
        gots = [rot_y(v, j + 1) for j, v in enumerate(send)]
        (last,) = call(sum_kernel, [(shape, BF)], (me_y, mine, *gots))
        sums.append(last)
        if k:
            last = rot_h(last, -k)
            back.append(last)
        for i in chunks:
            home[i].append(last)
    by = lax.rem(me_head + n_head - me_h, n_head).reshape(1)
    pieces = []
    for i in range(CHUNKS):
        ready = call(
            functools.partial(turn_kernel, n_head, i),
            [((r, piece, width), BF)] * n_head,
            (by, *home[i]),
        )
        pieces.append(ready[0])
        pieces.extend(rot_head(ready[j], j) for j in range(1, n_head))
    (out,) = call(
        functools.partial(gather_kernel, n_head),
        [((rows, r * 2 * width), BF)],
        (jnp.stack([me_head, me_b]), *pieces),
    )
    return out


def solution(mesh):
    placed = (
        P("seq", "head"),
        P("seq", "head"),
        P("seq", "head", None),
        P("seq", "head", None),
        P("seq", "head"),
        P("head"),
        P("head", "seq"),
    )
    return jax.shard_map(
        body, mesh=mesh, in_specs=placed, out_specs=P("seq", "head"), check_vma=False
    )
```

```python
import functools
import jax
import jax.numpy as jnp
from jax import lax
from jax.experimental import pallas as pl
from jax.experimental.pallas import tpu as pltpu
from jax.sharding import PartitionSpec as P

BF = jnp.bfloat16
F32 = jnp.float32
HIGH = lax.Precision.HIGHEST
TAIL = 16
CHUNKS = 2
MINE, OTHER, EARLY = (4, 4), (3, 2, 3), 3


def call(kernel, out_shapes, args, scratch=(), traffic=1, resident=0):
    vmem = pl.BlockSpec(memory_space=pltpu.VMEM)
    any_ = pl.BlockSpec()
    smem = pl.BlockSpec(memory_space=pltpu.SMEM)
    outs = pl.pallas_call(
        kernel,
        out_shape=[jax.ShapeDtypeStruct(s, d) for s, d in out_shapes],
        in_specs=[smem] + [any_] * (len(args) - 1 - resident) + [vmem] * resident,
        out_specs=[any_] * len(out_shapes),
        scratch_shapes=list(scratch),
        compiler_params=pltpu.CompilerParams(vmem_limit_bytes=16 << 20),
        cost_estimate=pl.CostEstimate(flops=1, transcendentals=0, bytes_accessed=traffic),
    )(*args)
    return list(outs)


def triangle(rows):
    i = lax.broadcasted_iota(jnp.int32, (rows, rows), 0)
    j = lax.broadcasted_iota(jnp.int32, (rows, rows), 1)
    return i >= j


def spread(per_head, channels):
    heads = per_head.shape[1]
    h = lax.broadcasted_iota(jnp.int32, (heads, channels), 0)
    c = lax.broadcasted_iota(jnp.int32, (heads, channels), 1)
    pick = (c // (channels // heads) == h).astype(F32)
    return jnp.dot(per_head, pick, precision=HIGH, preferred_element_type=F32)


def write_message(ref, state, decay):
    n, w = state.shape
    ref[0:n, :] = state.astype(BF)
    high = decay.astype(BF).astype(F32)
    row = lax.broadcasted_iota(jnp.int32, (TAIL, w), 0)
    tail = jnp.where(row < TAIL // 2, high, decay - high)
    ref[n : n + TAIL, :] = tail.astype(BF)


def read_message(ref):
    n = ref.shape[0] - TAIL
    tail = ref[n : n + TAIL, :].astype(F32)
    return ref[0:n, :].astype(F32), tail[0:1] + tail[TAIL // 2 : TAIL // 2 + 1]


def state_kernel(r, me, x, b, logs, keep, *sends):
    rows, channels = x.shape
    tri = triangle(rows).astype(F32)
    cum = jnp.dot(tri, logs[...], precision=HIGH, preferred_element_type=F32)
    total = cum[rows - 1 : rows, :]
    weights = spread(jnp.exp(total - cum), channels)
    decay = spread(jnp.broadcast_to(jnp.exp(total), (8, total.shape[1])), channels)[0:1]
    scaled = (weights * x[...].astype(F32)).astype(BF)
    state = lax.dot_general(b[...], scaled, (((0,), (0,)), ((), ())), preferred_element_type=F32)
    w = channels // r
    for g in range(r):

        @pl.when(me[0] == g)
        def _():
            for j, ref in enumerate((keep,) + sends):
                at = (g + j) % r * w
                write_message(ref, state[:, at : at + w], decay[:, at : at + w])


def fold_kernel(r, me, *refs):
    got, (message, run, run_decay) = refs[:r], refs[r:]
    for g in range(r):

        @pl.when(me[0] == g)
        def _():
            total, decay = read_message(got[g])
            for i in range(1, r):
                s, d = read_message(got[(g - i) % r])
                total, decay = total * d + s, decay * d
            write_message(message, total, decay)
            run[...] = total
            run_decay[...] = jnp.broadcast_to(decay, run_decay.shape)


def step_kernel(first, me, got, before, before_decay, run, run_decay, *refs):
    message, o_before, o_before_decay, o_run, o_run_decay = refs[-5:]
    s, d = read_message(got)
    if first:
        o_before[...], o_before_decay[...] = s, jnp.broadcast_to(d, o_before_decay.shape)
    else:
        o_before[...] = before[...] + before_decay[0:1] * s
        o_before_decay[...] = before_decay[...] * d
    total = run[...] + run_decay[0:1] * s
    decay = run_decay[0:1] * d
    write_message(message, total, decay)
    o_run[...] = total
    o_run_decay[...] = jnp.broadcast_to(decay, o_run_decay.shape)


def enter_kernel(r, me, got, before, before_decay, *refs):
    blocks, outs = refs[:r], refs[r:]
    s, _ = read_message(got)
    start = before[...] + before_decay[0:1] * s
    for g in range(r):

        @pl.when(me[0] == g)
        def _():
            now = start
            for i in range(r):
                outs[(i - g) % r][...] = now.astype(BF)
                if i + 1 < r:
                    q, d = read_message(blocks[(g - i) % r])
                    now = now * d + q


def within_kernel(me, x, z, b, c, logs, y, silu, grow):
    rows, channels = x.shape
    heads = logs.shape[1]
    width = channels // heads
    causal = triangle(rows)
    tri = causal.astype(F32)
    cum = jnp.dot(tri, logs[...], precision=HIGH, preferred_element_type=F32)
    cum_t = lax.dot_general(
        logs[...], tri, (((0,), (1,)), ((), ())), precision=HIGH, preferred_element_type=F32
    )
    scores = lax.dot_general(
        c[...], b[...], (((1,), (1,)), ((), ())), preferred_element_type=F32
    )
    scores = jnp.where(causal, scores, 0.0)
    for h in range(heads):
        diff = cum[:, h : h + 1] - cum_t[h : h + 1, :]
        mask = jnp.exp(jnp.where(causal, diff, 0.0))
        weighted = (mask * scores).astype(BF)
        at = slice(h * width, (h + 1) * width)
        y[:, at] = jnp.dot(weighted, x[:, at], preferred_element_type=F32)
    gate = z[...].astype(F32)
    silu[...] = gate / (1.0 + jnp.exp(-gate))
    grow[...] = spread(jnp.exp(cum), channels)


def hidden_kernel(r, me, c, y, silu, grow, gain, *refs):
    parts, outs, entering = refs[:r], refs[-1 - CHUNKS : -1], refs[-1]
    w = entering.shape[1] // r
    for g in range(r):

        @pl.when(me[0] == g)
        def _():
            for j in range(r):
                at = (g - j) % r * w
                entering[:, at : at + w] = parts[j][...]

    rows = c.shape[0] // len(outs)
    for i, out in enumerate(outs):
        at = slice(i * rows, (i + 1) * rows)
        carried = jnp.dot(c[at, :], entering[...], preferred_element_type=F32)
        gated = (y[at, :] + grow[at, :] * carried) * silu[at, :]
        mean_sq = jnp.mean(gated * gated, axis=1, keepdims=True)
        out[...] = (gated * lax.rsqrt(mean_sq + 1e-05) * gain[...]).astype(BF)


def split_kernel(n_mine, core, w_out, *refs):
    width = refs[0].shape[1]
    for g in range(2):

        @pl.when(core[0] == g)
        def _():
            for parts, side in ((refs[:n_mine], g), (refs[n_mine:], 1 - g)):
                at = 0
                for ref in parts:
                    rows = ref.shape[0]
                    ref[...] = w_out[at : at + rows, side * width : (side + 1) * width]
                    at += rows


def product_kernel(r, n_y, chunks, me, *refs):
    rows = [jnp.concatenate([ref[...] for ref in refs[i * chunks : (i + 1) * chunks]]) for i in range(2)]
    weights, (mine, *sends) = refs[2 * chunks : -n_y], refs[-n_y:]
    per = len(weights) // r
    shares = [ref.shape[0] for ref in weights[:per]]
    half = rows[0].shape[0] // chunks
    part = half // n_y
    for p in range(r):
        term, side, at = None, 0, 0
        for ref, share in zip(weights[p * per : (p + 1) * per], shares):
            one = jnp.dot(
                rows[side][:, at : at + share], ref[...], preferred_element_type=F32
            )
            term = one if term is None else term + one
            at += share
            if at == rows[0].shape[1]:
                side, at = 1, 0
        for g in range(n_y):

            @pl.when(me[0] == g)
            def _():
                for i in range(chunks):
                    at = i * half + g * part
                    mine[i, p] = term[at : at + part]
                    for j, ref in enumerate(sends):
                        at = i * half + (g + j + 1) % n_y * part
                        ref[i, p] = term[at : at + part].astype(BF)


def sum_kernel(me, mine, *refs):
    gots, out = refs[:-1], refs[-1]
    total = mine[...]
    for got in gots:
        total = total + got[...].astype(F32)
    out[...] = total.astype(BF)


def turn_kernel(n, chunk, by, *refs):
    ins, outs = refs[:n], refs[n:]
    for g in range(n):

        @pl.when(by[0] == g)
        def _():
            for j in range(n):
                ref = ins[(g + j) % n]
                outs[j][...] = ref[chunk if ref.shape[0] > 1 else 0]


def gather_kernel(n, me, *refs):
    ins, out = refs[:-1], refs[-1]
    r, part, width = ins[0].shape
    for t, ref in enumerate(ins):
        i, j = t // n, t % n
        source = lax.rem(me[0] + n - j, n)
        row = i * (n // 2) * part + lax.div(source, 2) * part
        row = pl.multiple_of(row, part)
        for p in range(r):
            order = lax.rem(me[1] + r - p, r)
            column = pl.multiple_of((2 * order + lax.rem(source, 2)) * width, width)
            out[pl.ds(row, part), pl.ds(column, width)] = ref[p]


def body(x_in, z_gate, b_proj, c_proj, log_decay, norm_gain, w_out):
    rows, channels = x_in.shape
    n_seq, n_head = lax.axis_size("seq"), lax.axis_size("head")
    r = n_seq // n_head
    n_y = n_head // 2
    me_seq, me_head = lax.axis_index("seq"), lax.axis_index("head")
    me_h, me_b = me_seq // r, me_seq % r
    me = me_b.reshape(1)

    def rot_b(v, j):
        pairs = [(h * r + b, h * r + (b + j) % r) for h in range(n_head) for b in range(r)]
        return lax.ppermute(v, "seq", pairs)

    def rot_h(v, k):
        pairs = [(h * r + b, (h + k) % n_head * r + b) for h in range(n_head) for b in range(r)]
        return lax.ppermute(v, "seq", pairs)

    def shift_h(v, k):
        pairs = [(h * r + b, (h + k) * r + b) for h in range(n_head - k) for b in range(r)]
        return lax.ppermute(v, "seq", pairs)

    def swap_core(v):
        return lax.ppermute(v, "head", [(i, i ^ 1) for i in range(n_head)])

    def rot_y(v, j):
        pairs = [(y * 2 + c, (y + j) % n_y * 2 + c) for y in range(n_y) for c in range(2)]
        return lax.ppermute(v, "head", pairs)

    def rot_head(v, j):
        return lax.ppermute(v, "head", [(i, (i + j) % n_head) for i in range(n_head)])

    pick = lambda v, i: lax.dynamic_index_in_dim(v, i, 0, keepdims=False)
    after = lambda v, *first: lax.optimization_barrier((v,) + first)[0]
    core = (me_head % 2).reshape(1)
    b_local = b_proj[:, 0, :]
    c_local = c_proj[:, 0, :]
    n = b_local.shape[1]
    w = channels // r
    message = ((n + TAIL, w), BF)
    full, row = ((n, w), F32), ((8, w), F32)

    sends = call(functools.partial(state_kernel, r), [message] * r, (me, x_in, b_local, log_decay))
    got = [sends[0]] + [rot_b(sends[j], j) for j in range(1, r)]
    depth, width = w_out.shape[0], w_out.shape[1] // 2
    mine_rows, other_rows = [[depth * i // 8 for i in cut] for cut in (MINE, OTHER)]
    split = call(
        functools.partial(split_kernel, len(mine_rows)),
        [((d, width), BF) for d in mine_rows + other_rows],
        (core, after(w_out, *sends)),
        traffic=4 * w_out.size * w_out.dtype.itemsize,
    )
    w_own = split[: len(mine_rows)] + [swap_core(v) for v in split[len(mine_rows) :]]
    w_parts = [w_own]
    for j in range(1, r):
        w_parts.append([rot_b(v, j) for v in w_own[:EARLY]])
    early = [v for group in w_parts[1:] for v in group]
    out, run, run_decay = call(functools.partial(fold_kernel, r), [message, full, row], (me, *got))
    before, before_decay = run, run_decay
    out = after(out, *split)
    k = 1
    while 2 * k < n_head:
        out, before, before_decay, run, run_decay = call(
            functools.partial(step_kernel, k == 1),
            [message, full, row, full, row],
            (me, shift_h(out, k), before, before_decay, run, run_decay, *got),
        )
        k *= 2
        out = after(out, *[group[0] for group in w_parts[1:]])
    entering = call(
        functools.partial(enter_kernel, r),
        [((n, w), BF)] * r,
        (me, shift_h(out, k), before, before_decay, *got),
    )
    parts = [entering[0]] + [rot_b(after(entering[j], *early), j) for j in range(1, r)]
    y, silu, grow = call(
        within_kernel,
        [((rows, channels), F32)] * 3,
        (me, x_in, after(z_gate, *entering), b_local, c_local, log_decay),
    )
    part_rows = rows // CHUNKS
    hidden = call(
        functools.partial(hidden_kernel, r),
        [((part_rows, channels), BF)] * CHUNKS,
        (me, c_local, y, silu, grow, norm_gain.reshape(1, channels), *parts, *early),
        scratch=[pltpu.VMEM((n, channels), BF)],
    )

    for j in range(1, r):
        w_parts[j].extend(rot_b(after(v, y), j) for v in w_own[EARLY:])
    weights = [v for group in w_parts for v in group]

    piece = part_rows // n_y
    me_y = (me_head // 2).reshape(1)
    steps = [(k, list(range(CHUNKS))) for k in range(n_head - 1)]
    steps += [(n_head - 1, [i]) for i in range(CHUNKS)]
    hidden = list(hidden)
    home, sums, back, outs = [[] for _ in range(CHUNKS)], [], [], []
    for t, (k, chunks) in enumerate(steps):
        now = [hidden[i] for i in chunks]
        if k + 1 < n_head:
            hidden = [rot_h(after(v, *outs[: max(t - 1, 0)]), 1) for v in hidden]
        other = [swap_core(v) for v in now]
        if t == 2:
            other[0] = after(other[0], sums[0])
        shape = (len(chunks), r, piece, width)
        mine, *send = call(
            functools.partial(product_kernel, r, n_y, len(chunks)),
            [(shape, F32)] + [(shape, BF)] * (n_y - 1),
            (me_y, *now, *other, *weights),
            resident=len(weights),
        )
        outs.append(mine)
        gots = [rot_y(v, j + 1) for j, v in enumerate(send)]
        (last,) = call(sum_kernel, [(shape, BF)], (me_y, mine, *gots))
        sums.append(last)
        if k:
            last = rot_h(last, -k)
            back.append(last)
        for i in chunks:
            home[i].append(last)
    by = lax.rem(me_head + n_head - me_h, n_head).reshape(1)
    pieces = []
    for i in range(CHUNKS):
        ready = call(
            functools.partial(turn_kernel, n_head, i),
            [((r, piece, width), BF)] * n_head,
            (by, *home[i]),
        )
        pieces.append(ready[0])
        pieces.extend(rot_head(ready[j], j) for j in range(1, n_head))
    (out,) = call(
        functools.partial(gather_kernel, n_head),
        [((rows, r * 2 * width), BF)],
        (jnp.stack([me_head, me_b]), *pieces),
    )
    return out


def solution(mesh):
    placed = (
        P("seq", "head"),
        P("seq", "head"),
        P("seq", "head", None),
        P("seq", "head", None),
        P("seq", "head"),
        P("head"),
        P("head", "seq"),
    )
    return jax.shard_map(
        body, mesh=mesh, in_specs=placed, out_specs=P("seq", "head"), check_vma=False
    )
```

```python
import functools
import jax
import jax.numpy as jnp
from jax import lax
from jax.experimental import pallas as pl
from jax.experimental.pallas import tpu as pltpu
from jax.sharding import PartitionSpec as P

BF = jnp.bfloat16
F32 = jnp.float32
HIGH = lax.Precision.HIGHEST
TAIL = 16
CHUNKS = 2
MINE, OTHER, EARLY = (4, 4), (3, 2, 3), 3


def call(kernel, out_shapes, args, scratch=(), traffic=1, resident=0):
    vmem = pl.BlockSpec(memory_space=pltpu.VMEM)
    any_ = pl.BlockSpec()
    smem = pl.BlockSpec(memory_space=pltpu.SMEM)
    outs = pl.pallas_call(
        kernel,
        out_shape=[jax.ShapeDtypeStruct(s, d) for s, d in out_shapes],
        in_specs=[smem] + [any_] * (len(args) - 1 - resident) + [vmem] * resident,
        out_specs=[any_] * len(out_shapes),
        scratch_shapes=list(scratch),
        compiler_params=pltpu.CompilerParams(vmem_limit_bytes=16 << 20),
        cost_estimate=pl.CostEstimate(flops=1, transcendentals=0, bytes_accessed=traffic),
    )(*args)
    return list(outs)


def triangle(rows):
    i = lax.broadcasted_iota(jnp.int32, (rows, rows), 0)
    j = lax.broadcasted_iota(jnp.int32, (rows, rows), 1)
    return i >= j


def spread(per_head, channels):
    heads = per_head.shape[1]
    h = lax.broadcasted_iota(jnp.int32, (heads, channels), 0)
    c = lax.broadcasted_iota(jnp.int32, (heads, channels), 1)
    pick = (c // (channels // heads) == h).astype(F32)
    return jnp.dot(per_head, pick, precision=HIGH, preferred_element_type=F32)


def write_message(ref, state, decay):
    n, w = state.shape
    ref[0:n, :] = state.astype(BF)
    high = decay.astype(BF).astype(F32)
    row = lax.broadcasted_iota(jnp.int32, (TAIL, w), 0)
    tail = jnp.where(row < TAIL // 2, high, decay - high)
    ref[n : n + TAIL, :] = tail.astype(BF)


def read_message(ref):
    n = ref.shape[0] - TAIL
    tail = ref[n : n + TAIL, :].astype(F32)
    return ref[0:n, :].astype(F32), tail[0:1] + tail[TAIL // 2 : TAIL // 2 + 1]


def state_kernel(r, me, x, b, logs, keep, *sends):
    rows, channels = x.shape
    tri = triangle(rows).astype(F32)
    cum = jnp.dot(tri, logs[...], precision=HIGH, preferred_element_type=F32)
    total = cum[rows - 1 : rows, :]
    weights = spread(jnp.exp(total - cum), channels)
    decay = spread(jnp.broadcast_to(jnp.exp(total), (8, total.shape[1])), channels)[0:1]
    scaled = (weights * x[...].astype(F32)).astype(BF)
    state = lax.dot_general(b[...], scaled, (((0,), (0,)), ((), ())), preferred_element_type=F32)
    w = channels // r
    for g in range(r):

        @pl.when(me[0] == g)
        def _():
            for j, ref in enumerate((keep,) + sends):
                at = (g + j) % r * w
                write_message(ref, state[:, at : at + w], decay[:, at : at + w])


def fold_kernel(r, me, *refs):
    got, (message, run, run_decay) = refs[:r], refs[r:]
    for g in range(r):

        @pl.when(me[0] == g)
        def _():
            total, decay = read_message(got[g])
            for i in range(1, r):
                s, d = read_message(got[(g - i) % r])
                total, decay = total * d + s, decay * d
            write_message(message, total, decay)
            run[...] = total
            run_decay[...] = jnp.broadcast_to(decay, run_decay.shape)


def step_kernel(first, me, got, before, before_decay, run, run_decay, *refs):
    message, o_before, o_before_decay, o_run, o_run_decay = refs[-5:]
    s, d = read_message(got)
    if first:
        o_before[...], o_before_decay[...] = s, jnp.broadcast_to(d, o_before_decay.shape)
    else:
        o_before[...] = before[...] + before_decay[0:1] * s
        o_before_decay[...] = before_decay[...] * d
    total = run[...] + run_decay[0:1] * s
    decay = run_decay[0:1] * d
    write_message(message, total, decay)
    o_run[...] = total
    o_run_decay[...] = jnp.broadcast_to(decay, o_run_decay.shape)


def enter_kernel(r, me, got, before, before_decay, *refs):
    blocks, outs = refs[:r], refs[r:]
    s, _ = read_message(got)
    start = before[...] + before_decay[0:1] * s
    for g in range(r):

        @pl.when(me[0] == g)
        def _():
            now = start
            for i in range(r):
                outs[(i - g) % r][...] = now.astype(BF)
                if i + 1 < r:
                    q, d = read_message(blocks[(g - i) % r])
                    now = now * d + q


def within_kernel(me, x, z, b, c, logs, y, silu, grow):
    rows, channels = x.shape
    heads = logs.shape[1]
    width = channels // heads
    causal = triangle(rows)
    tri = causal.astype(F32)
    cum = jnp.dot(tri, logs[...], precision=HIGH, preferred_element_type=F32)
    cum_t = lax.dot_general(
        logs[...], tri, (((0,), (1,)), ((), ())), precision=HIGH, preferred_element_type=F32
    )
    scores = lax.dot_general(
        c[...], b[...], (((1,), (1,)), ((), ())), preferred_element_type=F32
    )
    scores = jnp.where(causal, scores, 0.0)
    for h in range(heads):
        diff = cum[:, h : h + 1] - cum_t[h : h + 1, :]
        mask = jnp.exp(jnp.where(causal, diff, 0.0))
        weighted = (mask * scores).astype(BF)
        at = slice(h * width, (h + 1) * width)
        y[:, at] = jnp.dot(weighted, x[:, at], preferred_element_type=F32)
    gate = z[...].astype(F32)
    silu[...] = gate / (1.0 + jnp.exp(-gate))
    grow[...] = spread(jnp.exp(cum), channels)


def hidden_kernel(r, me, c, y, silu, grow, gain, *refs):
    parts, outs, entering = refs[:r], refs[-1 - CHUNKS : -1], refs[-1]
    w = entering.shape[1] // r
    for g in range(r):

        @pl.when(me[0] == g)
        def _():
            for j in range(r):
                at = (g - j) % r * w
                entering[:, at : at + w] = parts[j][...]

    rows = c.shape[0] // len(outs)
    for i, out in enumerate(outs):
        at = slice(i * rows, (i + 1) * rows)
        carried = jnp.dot(c[at, :], entering[...], preferred_element_type=F32)
        gated = (y[at, :] + grow[at, :] * carried) * silu[at, :]
        mean_sq = jnp.mean(gated * gated, axis=1, keepdims=True)
        out[...] = (gated * lax.rsqrt(mean_sq + 1e-05) * gain[...]).astype(BF)


def split_kernel(n_mine, core, w_out, *refs):
    width = refs[0].shape[1]
    for g in range(2):

        @pl.when(core[0] == g)
        def _():
            for parts, side in ((refs[:n_mine], g), (refs[n_mine:], 1 - g)):
                at = 0
                for ref in parts:
                    rows = ref.shape[0]
                    ref[...] = w_out[at : at + rows, side * width : (side + 1) * width]
                    at += rows


def product_kernel(r, n_y, chunks, me, *refs):
    rows = [jnp.concatenate([ref[...] for ref in refs[i * chunks : (i + 1) * chunks]]) for i in range(2)]
    weights, (mine, *sends) = refs[2 * chunks : -n_y], refs[-n_y:]
    per = len(weights) // r
    shares = [ref.shape[0] for ref in weights[:per]]
    half = rows[0].shape[0] // chunks
    part = half // n_y
    for p in range(r):
        term, side, at = None, 0, 0
        for ref, share in zip(weights[p * per : (p + 1) * per], shares):
            one = jnp.dot(
                rows[side][:, at : at + share], ref[...], preferred_element_type=F32
            )
            term = one if term is None else term + one
            at += share
            if at == rows[0].shape[1]:
                side, at = 1, 0
        for g in range(n_y):

            @pl.when(me[0] == g)
            def _():
                for i in range(chunks):
                    at = i * half + g * part
                    mine[i, p] = term[at : at + part]
                    for j, ref in enumerate(sends):
                        at = i * half + (g + j + 1) % n_y * part
                        ref[i, p] = term[at : at + part].astype(BF)


def sum_kernel(me, mine, *refs):
    gots, out = refs[:-1], refs[-1]
    total = mine[...]
    for got in gots:
        total = total + got[...].astype(F32)
    out[...] = total.astype(BF)


def turn_kernel(n, chunk, by, *refs):
    ins, outs = refs[:n], refs[n:]
    for g in range(n):

        @pl.when(by[0] == g)
        def _():
            for j in range(n):
                ref = ins[(g + j) % n]
                outs[j][...] = ref[chunk if ref.shape[0] > 1 else 0]


def gather_kernel(n, me, *refs):
    ins, out = refs[:-1], refs[-1]
    r, part, width = ins[0].shape
    for t, ref in enumerate(ins):
        i, j = t // n, t % n
        source = lax.rem(me[0] + n - j, n)
        row = i * (n // 2) * part + lax.div(source, 2) * part
        row = pl.multiple_of(row, part)
        for p in range(r):
            order = lax.rem(me[1] + r - p, r)
            column = pl.multiple_of((2 * order + lax.rem(source, 2)) * width, width)
            out[pl.ds(row, part), pl.ds(column, width)] = ref[p]


def body(x_in, z_gate, b_proj, c_proj, log_decay, norm_gain, w_out):
    rows, channels = x_in.shape
    n_seq, n_head = lax.axis_size("seq"), lax.axis_size("head")
    r = n_seq // n_head
    n_y = n_head // 2
    me_seq, me_head = lax.axis_index("seq"), lax.axis_index("head")
    me_h, me_b = me_seq // r, me_seq % r
    me = me_b.reshape(1)

    def rot_b(v, j):
        pairs = [(h * r + b, h * r + (b + j) % r) for h in range(n_head) for b in range(r)]
        return lax.ppermute(v, "seq", pairs)

    def rot_h(v, k):
        pairs = [(h * r + b, (h + k) % n_head * r + b) for h in range(n_head) for b in range(r)]
        return lax.ppermute(v, "seq", pairs)

    def shift_h(v, k):
        pairs = [(h * r + b, (h + k) * r + b) for h in range(n_head - k) for b in range(r)]
        return lax.ppermute(v, "seq", pairs)

    def swap_core(v):
        return lax.ppermute(v, "head", [(i, i ^ 1) for i in range(n_head)])

    def rot_y(v, j):
        pairs = [(y * 2 + c, (y + j) % n_y * 2 + c) for y in range(n_y) for c in range(2)]
        return lax.ppermute(v, "head", pairs)

    def rot_head(v, j):
        return lax.ppermute(v, "head", [(i, (i + j) % n_head) for i in range(n_head)])

    pick = lambda v, i: lax.dynamic_index_in_dim(v, i, 0, keepdims=False)
    after = lambda v, *first: lax.optimization_barrier((v,) + first)[0]
    core = (me_head % 2).reshape(1)
    b_local = b_proj[:, 0, :]
    c_local = c_proj[:, 0, :]
    n = b_local.shape[1]
    w = channels // r
    message = ((n + TAIL, w), BF)
    full, row = ((n, w), F32), ((8, w), F32)

    sends = call(functools.partial(state_kernel, r), [message] * r, (me, x_in, b_local, log_decay))
    got = [sends[0]] + [rot_b(sends[j], j) for j in range(1, r)]
    depth, width = w_out.shape[0], w_out.shape[1] // 2
    mine_rows, other_rows = [[depth * i // 8 for i in cut] for cut in (MINE, OTHER)]
    split = call(
        functools.partial(split_kernel, len(mine_rows)),
        [((d, width), BF) for d in mine_rows + other_rows],
        (core, after(w_out, *sends)),
        traffic=4 * w_out.size * w_out.dtype.itemsize,
    )
    w_own = split[: len(mine_rows)] + [swap_core(v) for v in split[len(mine_rows) :]]
    w_parts = [w_own]
    for j in range(1, r):
        w_parts.append([rot_b(v, j) for v in w_own[:EARLY]])
    early = [v for group in w_parts[1:] for v in group]
    out, run, run_decay = call(functools.partial(fold_kernel, r), [message, full, row], (me, *got))
    before, before_decay = run, run_decay
    out = after(out, *split)
    k = 1
    while 2 * k < n_head:
        out, before, before_decay, run, run_decay = call(
            functools.partial(step_kernel, k == 1),
            [message, full, row, full, row],
            (me, shift_h(out, k), before, before_decay, run, run_decay, *got),
        )
        k *= 2
        out = after(out, *[group[0] for group in w_parts[1:]])
    entering = call(
        functools.partial(enter_kernel, r),
        [((n, w), BF)] * r,
        (me, shift_h(out, k), before, before_decay, *got),
    )
    parts = [entering[0]] + [rot_b(after(entering[j], *early), j) for j in range(1, r)]
    y, silu, grow = call(
        within_kernel,
        [((rows, channels), F32)] * 3,
        (me, x_in, after(z_gate, *entering), b_local, c_local, log_decay),
    )
    part_rows = rows // CHUNKS
    hidden = call(
        functools.partial(hidden_kernel, r),
        [((part_rows, channels), BF)] * CHUNKS,
        (me, c_local, y, silu, grow, norm_gain.reshape(1, channels), *parts, *early),
        scratch=[pltpu.VMEM((n, channels), BF)],
    )

    for j in range(1, r):
        w_parts[j].extend(rot_b(after(v, y), j) for v in w_own[EARLY:])
    weights = [v for group in w_parts for v in group]

    piece = part_rows // n_y
    me_y = (me_head // 2).reshape(1)
    steps = [(k, list(range(CHUNKS))) for k in range(n_head - 1)]
    steps += [(n_head - 1, [i]) for i in range(CHUNKS)]
    hidden = list(hidden)
    home, sums, back, outs = [[] for _ in range(CHUNKS)], [], [], []
    for t, (k, chunks) in enumerate(steps):
        now = [hidden[i] for i in chunks]
        if k + 1 < n_head:
            hidden = [rot_h(after(v, *outs[: max(t - 1, 0)]), 1) for v in hidden]
        other = [swap_core(v) for v in now]
        if t > 3:
            other[0] = after(other[0], sums[t - 4])
        shape = (len(chunks), r, piece, width)
        mine, *send = call(
            functools.partial(product_kernel, r, n_y, len(chunks)),
            [(shape, F32)] + [(shape, BF)] * (n_y - 1),
            (me_y, *now, *other, *weights),
            resident=len(weights),
        )
        outs.append(mine)
        gots = [rot_y(v, j + 1) for j, v in enumerate(send)]
        (last,) = call(sum_kernel, [(shape, BF)], (me_y, mine, *gots))
        sums.append(last)
        if k:
            last = rot_h(last, -k)
            back.append(last)
        for i in chunks:
            home[i].append(last)
    by = lax.rem(me_head + n_head - me_h, n_head).reshape(1)
    pieces = []
    for i in range(CHUNKS):
        ready = call(
            functools.partial(turn_kernel, n_head, i),
            [((r, piece, width), BF)] * n_head,
            (by, *home[i]),
        )
        pieces.append(ready[0])
        pieces.extend(rot_head(ready[j], j) for j in range(1, n_head))
    (out,) = call(
        functools.partial(gather_kernel, n_head),
        [((rows, r * 2 * width), BF)],
        (jnp.stack([me_head, me_b]), *pieces),
    )
    return out


def solution(mesh):
    placed = (
        P("seq", "head"),
        P("seq", "head"),
        P("seq", "head", None),
        P("seq", "head", None),
        P("seq", "head"),
        P("head"),
        P("head", "seq"),
    )
    return jax.shard_map(
        body, mesh=mesh, in_specs=placed, out_specs=P("seq", "head"), check_vma=False
    )
```

```python
import functools
import jax
import jax.numpy as jnp
from jax import lax
from jax.experimental import pallas as pl
from jax.experimental.pallas import tpu as pltpu
from jax.sharding import PartitionSpec as P

BF = jnp.bfloat16
F32 = jnp.float32
HIGH = lax.Precision.HIGHEST
TAIL = 16
CHUNKS = 2
MINE, OTHER, EARLY = (4, 4), (3, 2, 3), 3


def call(kernel, out_shapes, args, scratch=(), traffic=1, resident=0):
    vmem = pl.BlockSpec(memory_space=pltpu.VMEM)
    any_ = pl.BlockSpec()
    smem = pl.BlockSpec(memory_space=pltpu.SMEM)
    outs = pl.pallas_call(
        kernel,
        out_shape=[jax.ShapeDtypeStruct(s, d) for s, d in out_shapes],
        in_specs=[smem] + [any_] * (len(args) - 1 - resident) + [vmem] * resident,
        out_specs=[any_] * len(out_shapes),
        scratch_shapes=list(scratch),
        compiler_params=pltpu.CompilerParams(vmem_limit_bytes=16 << 20),
        cost_estimate=pl.CostEstimate(flops=1, transcendentals=0, bytes_accessed=traffic),
    )(*args)
    return list(outs)


def triangle(rows):
    i = lax.broadcasted_iota(jnp.int32, (rows, rows), 0)
    j = lax.broadcasted_iota(jnp.int32, (rows, rows), 1)
    return i >= j


def spread(per_head, channels):
    heads = per_head.shape[1]
    h = lax.broadcasted_iota(jnp.int32, (heads, channels), 0)
    c = lax.broadcasted_iota(jnp.int32, (heads, channels), 1)
    pick = (c // (channels // heads) == h).astype(F32)
    return jnp.dot(per_head, pick, precision=HIGH, preferred_element_type=F32)


def write_message(ref, state, decay):
    n, w = state.shape
    ref[0:n, :] = state.astype(BF)
    high = decay.astype(BF).astype(F32)
    row = lax.broadcasted_iota(jnp.int32, (TAIL, w), 0)
    tail = jnp.where(row < TAIL // 2, high, decay - high)
    ref[n : n + TAIL, :] = tail.astype(BF)


def read_message(ref):
    n = ref.shape[0] - TAIL
    tail = ref[n : n + TAIL, :].astype(F32)
    return ref[0:n, :].astype(F32), tail[0:1] + tail[TAIL // 2 : TAIL // 2 + 1]


def state_kernel(r, me, x, b, logs, keep, *sends):
    rows, channels = x.shape
    tri = triangle(rows).astype(F32)
    cum = jnp.dot(tri, logs[...], precision=HIGH, preferred_element_type=F32)
    total = cum[rows - 1 : rows, :]
    weights = spread(jnp.exp(total - cum), channels)
    decay = spread(jnp.broadcast_to(jnp.exp(total), (8, total.shape[1])), channels)[0:1]
    scaled = (weights * x[...].astype(F32)).astype(BF)
    state = lax.dot_general(b[...], scaled, (((0,), (0,)), ((), ())), preferred_element_type=F32)
    w = channels // r
    for g in range(r):

        @pl.when(me[0] == g)
        def _():
            for j, ref in enumerate((keep,) + sends):
                at = (g + j) % r * w
                write_message(ref, state[:, at : at + w], decay[:, at : at + w])


def fold_kernel(r, me, *refs):
    got, (message, run, run_decay) = refs[:r], refs[r:]
    for g in range(r):

        @pl.when(me[0] == g)
        def _():
            total, decay = read_message(got[g])
            for i in range(1, r):
                s, d = read_message(got[(g - i) % r])
                total, decay = total * d + s, decay * d
            write_message(message, total, decay)
            run[...] = total
            run_decay[...] = jnp.broadcast_to(decay, run_decay.shape)


def step_kernel(first, me, got, before, before_decay, run, run_decay, *refs):
    message, o_before, o_before_decay, o_run, o_run_decay = refs[-5:]
    s, d = read_message(got)
    if first:
        o_before[...], o_before_decay[...] = s, jnp.broadcast_to(d, o_before_decay.shape)
    else:
        o_before[...] = before[...] + before_decay[0:1] * s
        o_before_decay[...] = before_decay[...] * d
    total = run[...] + run_decay[0:1] * s
    decay = run_decay[0:1] * d
    write_message(message, total, decay)
    o_run[...] = total
    o_run_decay[...] = jnp.broadcast_to(decay, o_run_decay.shape)


def enter_kernel(r, me, got, before, before_decay, *refs):
    blocks, outs = refs[:r], refs[r:]
    s, _ = read_message(got)
    start = before[...] + before_decay[0:1] * s
    for g in range(r):

        @pl.when(me[0] == g)
        def _():
            now = start
            for i in range(r):
                outs[(i - g) % r][...] = now.astype(BF)
                if i + 1 < r:
                    q, d = read_message(blocks[(g - i) % r])
                    now = now * d + q


def within_kernel(me, x, z, b, c, logs, y, silu, grow):
    rows, channels = x.shape
    heads = logs.shape[1]
    width = channels // heads
    causal = triangle(rows)
    tri = causal.astype(F32)
    cum = jnp.dot(tri, logs[...], precision=HIGH, preferred_element_type=F32)
    cum_t = lax.dot_general(
        logs[...], tri, (((0,), (1,)), ((), ())), precision=HIGH, preferred_element_type=F32
    )
    scores = lax.dot_general(
        c[...], b[...], (((1,), (1,)), ((), ())), preferred_element_type=F32
    )
    scores = jnp.where(causal, scores, 0.0)
    for h in range(heads):
        diff = cum[:, h : h + 1] - cum_t[h : h + 1, :]
        mask = jnp.exp(jnp.where(causal, diff, 0.0))
        weighted = (mask * scores).astype(BF)
        at = slice(h * width, (h + 1) * width)
        y[:, at] = jnp.dot(weighted, x[:, at], preferred_element_type=F32)
    gate = z[...].astype(F32)
    silu[...] = gate / (1.0 + jnp.exp(-gate))
    grow[...] = spread(jnp.exp(cum), channels)


def hidden_kernel(r, me, c, y, silu, grow, gain, *refs):
    parts, outs, entering = refs[:r], refs[-1 - CHUNKS : -1], refs[-1]
    w = entering.shape[1] // r
    for g in range(r):

        @pl.when(me[0] == g)
        def _():
            for j in range(r):
                at = (g - j) % r * w
                entering[:, at : at + w] = parts[j][...]

    rows = c.shape[0] // len(outs)
    for i, out in enumerate(outs):
        at = slice(i * rows, (i + 1) * rows)
        carried = jnp.dot(c[at, :], entering[...], preferred_element_type=F32)
        gated = (y[at, :] + grow[at, :] * carried) * silu[at, :]
        mean_sq = jnp.mean(gated * gated, axis=1, keepdims=True)
        out[...] = (gated * lax.rsqrt(mean_sq + 1e-05) * gain[...]).astype(BF)


def split_kernel(n_mine, core, w_out, *refs):
    width = refs[0].shape[1]
    for g in range(2):

        @pl.when(core[0] == g)
        def _():
            for parts, side in ((refs[:n_mine], g), (refs[n_mine:], 1 - g)):
                at = 0
                for ref in parts:
                    rows = ref.shape[0]
                    ref[...] = w_out[at : at + rows, side * width : (side + 1) * width]
                    at += rows


def product_kernel(r, n_y, chunks, me, *refs):
    rows = [jnp.concatenate([ref[...] for ref in refs[i * chunks : (i + 1) * chunks]]) for i in range(2)]
    weights, (mine, *sends) = refs[2 * chunks : -n_y], refs[-n_y:]
    per = len(weights) // r
    shares = [ref.shape[0] for ref in weights[:per]]
    half = rows[0].shape[0] // chunks
    part = half // n_y
    for p in range(r):
        term, side, at = None, 0, 0
        for ref, share in zip(weights[p * per : (p + 1) * per], shares):
            one = jnp.dot(
                rows[side][:, at : at + share], ref[...], preferred_element_type=F32
            )
            term = one if term is None else term + one
            at += share
            if at == rows[0].shape[1]:
                side, at = 1, 0
        for g in range(n_y):

            @pl.when(me[0] == g)
            def _():
                for i in range(chunks):
                    at = i * half + g * part
                    mine[i, p] = term[at : at + part]
                    for j, ref in enumerate(sends):
                        at = i * half + (g + j + 1) % n_y * part
                        ref[i, p] = term[at : at + part].astype(BF)


def sum_kernel(me, mine, *refs):
    gots, out = refs[:-1], refs[-1]
    total = mine[...]
    for got in gots:
        total = total + got[...].astype(F32)
    out[...] = total.astype(BF)


def turn_kernel(n, chunk, by, *refs):
    ins, outs = refs[:n], refs[n:]
    for g in range(n):

        @pl.when(by[0] == g)
        def _():
            for j in range(n):
                ref = ins[(g + j) % n]
                outs[j][...] = ref[chunk if ref.shape[0] > 1 else 0]


def gather_kernel(n, me, *refs):
    ins, out = refs[:-1], refs[-1]
    r, part, width = ins[0].shape
    for t, ref in enumerate(ins):
        i, j = t // n, t % n
        source = lax.rem(me[0] + n - j, n)
        row = i * (n // 2) * part + lax.div(source, 2) * part
        row = pl.multiple_of(row, part)
        for p in range(r):
            order = lax.rem(me[1] + r - p, r)
            column = pl.multiple_of((2 * order + lax.rem(source, 2)) * width, width)
            out[pl.ds(row, part), pl.ds(column, width)] = ref[p]


def body(x_in, z_gate, b_proj, c_proj, log_decay, norm_gain, w_out):
    rows, channels = x_in.shape
    n_seq, n_head = lax.axis_size("seq"), lax.axis_size("head")
    r = n_seq // n_head
    n_y = n_head // 2
    me_seq, me_head = lax.axis_index("seq"), lax.axis_index("head")
    me_h, me_b = me_seq // r, me_seq % r
    me = me_b.reshape(1)

    def rot_b(v, j):
        pairs = [(h * r + b, h * r + (b + j) % r) for h in range(n_head) for b in range(r)]
        return lax.ppermute(v, "seq", pairs)

    def rot_h(v, k):
        pairs = [(h * r + b, (h + k) % n_head * r + b) for h in range(n_head) for b in range(r)]
        return lax.ppermute(v, "seq", pairs)

    def shift_h(v, k):
        pairs = [(h * r + b, (h + k) * r + b) for h in range(n_head - k) for b in range(r)]
        return lax.ppermute(v, "seq", pairs)

    def swap_core(v):
        return lax.ppermute(v, "head", [(i, i ^ 1) for i in range(n_head)])

    def rot_y(v, j):
        pairs = [(y * 2 + c, (y + j) % n_y * 2 + c) for y in range(n_y) for c in range(2)]
        return lax.ppermute(v, "head", pairs)

    def rot_head(v, j):
        return lax.ppermute(v, "head", [(i, (i + j) % n_head) for i in range(n_head)])

    pick = lambda v, i: lax.dynamic_index_in_dim(v, i, 0, keepdims=False)
    after = lambda v, *first: lax.optimization_barrier((v,) + first)[0]
    core = (me_head % 2).reshape(1)
    b_local = b_proj[:, 0, :]
    c_local = c_proj[:, 0, :]
    n = b_local.shape[1]
    w = channels // r
    message = ((n + TAIL, w), BF)
    full, row = ((n, w), F32), ((8, w), F32)

    sends = call(functools.partial(state_kernel, r), [message] * r, (me, x_in, b_local, log_decay))
    got = [sends[0]] + [rot_b(sends[j], j) for j in range(1, r)]
    depth, width = w_out.shape[0], w_out.shape[1] // 2
    mine_rows, other_rows = [[depth * i // 8 for i in cut] for cut in (MINE, OTHER)]
    split = call(
        functools.partial(split_kernel, len(mine_rows)),
        [((d, width), BF) for d in mine_rows + other_rows],
        (core, after(w_out, *sends)),
        traffic=4 * w_out.size * w_out.dtype.itemsize,
    )
    w_own = split[: len(mine_rows)] + [swap_core(v) for v in split[len(mine_rows) :]]
    w_parts = [w_own]
    for j in range(1, r):
        w_parts.append([rot_b(v, j) for v in w_own[:EARLY]])
    early = [v for group in w_parts[1:] for v in group]
    out, run, run_decay = call(functools.partial(fold_kernel, r), [message, full, row], (me, *got))
    before, before_decay = run, run_decay
    out = after(out, *split)
    k = 1
    while 2 * k < n_head:
        out, before, before_decay, run, run_decay = call(
            functools.partial(step_kernel, k == 1),
            [message, full, row, full, row],
            (me, shift_h(out, k), before, before_decay, run, run_decay, *got),
        )
        k *= 2
        out = after(out, *[group[0] for group in w_parts[1:]])
    entering = call(
        functools.partial(enter_kernel, r),
        [((n, w), BF)] * r,
        (me, shift_h(out, k), before, before_decay, *got),
    )
    parts = [entering[0]] + [rot_b(after(entering[j], *early), j) for j in range(1, r)]
    y, silu, grow = call(
        within_kernel,
        [((rows, channels), F32)] * 3,
        (me, x_in, after(z_gate, *entering), b_local, c_local, log_decay),
    )
    part_rows = rows // CHUNKS
    hidden = call(
        functools.partial(hidden_kernel, r),
        [((part_rows, channels), BF)] * CHUNKS,
        (me, c_local, y, silu, grow, norm_gain.reshape(1, channels), *parts, *early),
        scratch=[pltpu.VMEM((n, channels), BF)],
    )

    for j in range(1, r):
        w_parts[j].extend(rot_b(after(v, y), j) for v in w_own[EARLY:])
    weights = [v for group in w_parts for v in group]

    piece = part_rows // n_y
    me_y = (me_head // 2).reshape(1)
    steps = [(k, list(range(CHUNKS))) for k in range(n_head - 1)]
    steps += [(n_head - 1, [i]) for i in range(CHUNKS)]
    hidden = list(hidden)
    home, sums, back, outs = [[] for _ in range(CHUNKS)], [], [], []
    for t, (k, chunks) in enumerate(steps):
        now = [hidden[i] for i in chunks]
        if k + 1 < n_head:
            hidden = [rot_h(after(v, *outs[: max(t - 1, 0)]), 1) for v in hidden]
        other = [swap_core(v) for v in now]
        if t > 2:
            other[0] = after(other[0], sums[1 if t == 3 else 0])
        shape = (len(chunks), r, piece, width)
        mine, *send = call(
            functools.partial(product_kernel, r, n_y, len(chunks)),
            [(shape, F32)] + [(shape, BF)] * (n_y - 1),
            (me_y, *now, *other, *weights),
        )
        outs.append(mine)
        gots = [rot_y(v, j + 1) for j, v in enumerate(send)]
        (last,) = call(sum_kernel, [(shape, BF)], (me_y, mine, *gots))
        sums.append(last)
        if k:
            last = rot_h(last, -k)
            back.append(last)
        for i in chunks:
            home[i].append(last)
    by = lax.rem(me_head + n_head - me_h, n_head).reshape(1)
    pieces = []
    for i in range(CHUNKS):
        ready = call(
            functools.partial(turn_kernel, n_head, i),
            [((r, piece, width), BF)] * n_head,
            (by, *home[i]),
        )
        pieces.append(ready[0])
        pieces.extend(rot_head(ready[j], j) for j in range(1, n_head))
    (out,) = call(
        functools.partial(gather_kernel, n_head),
        [((rows, r * 2 * width), BF)],
        (jnp.stack([me_head, me_b]), *pieces),
    )
    return out


def solution(mesh):
    placed = (
        P("seq", "head"),
        P("seq", "head"),
        P("seq", "head", None),
        P("seq", "head", None),
        P("seq", "head"),
        P("head"),
        P("head", "seq"),
    )
    return jax.shard_map(
        body, mesh=mesh, in_specs=placed, out_specs=P("seq", "head"), check_vma=False
    )
```
